128 devices in a mesh: ex: 16 (over z, y), feat: 8 (over x, core).
Axes of the slice: x: 4, y: 4, z: 4, core: 2. Of those that a mesh axis runs over, the one named last changes fastest.
Arguments:
- tiles: bfloat16 [16, 8, 384, 128, 128], P('ex', 'feat'), may hold values from -0.5 to 0.5
- row_index: int32 [16, 8, 384], P('ex', 'feat'), may hold values from 0 to 2047
- col_index: int32 [16, 8, 384], P('ex', 'feat'), may hold values from 0 to 4095
- weights: bfloat16 [32768, 128], P('feat'), may hold values from -6 to 6
- val_grad: float32 [32768, 128], P('feat'), may hold values from -6 to 6
- field_map: int32 [32768, 128], P('feat'), may hold values from 0 to 63
- field_lambda: float32 [64], replicated, may hold values from 0.05 to 2
Outputs:
- solution: float32 [32768, 128], P(('feat', 'ex'))
- hypergrad: float32 [64], replicated
The draws below stay inside these ranges and needn't reach their ends.
Inputs may be any that keep to these rules, and one draw needn't show every extreme that they name: `row_index`: local row tile of a stored tile within its device's 2048 row tiles. `col_index`: local column tile of a stored tile within its device's 4096 column tiles.
All inputs are finite; a program needn't handle non-finite values.
Results may differ from the reference program's by a relative error of at most 0.0021.
Values may be sent and summed in bfloat16 or wider, within the bound.
A program may use at most 128 MiB of HBM per device.

```python
import math
import jax
import jax.numpy as jnp
from jax import lax

TB = 128
RT_DEV = 2048
CT_DEV = 4096
TILES_DEV = 384
FIELDS = 64
ITERS = 3
RT = 32768
CT = 32768
NFEAT = 4194304
N_EX = 16
N_FEAT = 8


def place_ends(result, stream_key, low, top_value):
    longest = result.shape.index(max(result.shape))
    spots = []
    for shift in (0, 1):
        where = [jax.random.randint(jax.random.fold_in(stream_key, axis), (), 0, length) for axis, length in enumerate(result.shape)]
        where[longest] = (where[longest] + shift) % result.shape[longest]
        spots.append(tuple(where))
    return result.at[spots[0]].set(low).at[spots[1]].set(top_value)


def shard_levels(own_key, extent, split, least, high):
    def one(axis_at, shards_of):
        draws = jax.random.uniform(jax.random.fold_in(jax.random.fold_in(own_key, 6), axis_at), (shards_of,), jnp.float32, least / len(split), high / len(split))
        return jnp.repeat(jnp.exp(draws), extent[axis_at] // shards_of).reshape((-1,) + (1,) * (len(extent) - axis_at - 1))

    loudness = one(*split[0])
    for cut in split[1:]:
        loudness = loudness * one(*cut)
    return loudness


def gaussian(stream_key, dims, spread, reach, split=(), kind=jnp.bfloat16):
    level = shard_levels(stream_key, dims, split, -0.22, 0.18) if split else 1.0
    drawn = jax.random.normal(stream_key, dims, jnp.float32) * spread * level
    return jnp.minimum(jnp.maximum(drawn, -reach), reach).astype(kind)


def setup_inputs(seed: int = 0) -> dict:
    key_of = jax.random.split(jax.random.key(seed), 8)
    return {
        "tiles": gaussian(key_of[0], (N_EX, N_FEAT, TILES_DEV, TB, TB), TB ** -0.5, 0.5, ((0, 16), (1, 8))),
        "row_index": place_ends(jax.random.randint(key_of[1], (N_EX, N_FEAT, TILES_DEV), 0, RT_DEV), jax.random.fold_in(key_of[1], 1), 0, RT_DEV - 1).astype(jnp.int32),
        "col_index": place_ends(jax.random.randint(key_of[2], (N_EX, N_FEAT, TILES_DEV), 0, CT_DEV), jax.random.fold_in(key_of[2], 1), 0, CT_DEV - 1).astype(jnp.int32),
        "weights": gaussian(key_of[3], (CT, TB), 1.0, 6.0, ((0, 8),)),
        "val_grad": gaussian(key_of[4], (CT, TB), 1.0, 6.0, ((0, 8),), jnp.float32),
        "field_map": place_ends(jax.random.randint(key_of[5], (CT, TB), 0, FIELDS), jax.random.fold_in(key_of[5], 1), 0, FIELDS - 1).astype(jnp.int32),
        "field_lambda": jnp.clip(jnp.exp(jax.random.uniform(key_of[6], (FIELDS,), jnp.float32, math.log(0.05), math.log(2.0))), 0.05, 2.0),
    }


def reference(tiles, row_index, col_index, weights, val_grad, field_map, field_lambda):
    blocks = N_EX * N_FEAT
    flat_tiles = tiles.reshape(blocks, TILES_DEV, TB, TB)
    glob_rows = (row_index + (jnp.arange(N_EX, dtype=jnp.int32) * RT_DEV)[:, None, None]).astype(jnp.int32).reshape(blocks, TILES_DEV)
    glob_cols = (col_index + (jnp.arange(N_FEAT, dtype=jnp.int32) * CT_DEV)[None, :, None]).astype(jnp.int32).reshape(blocks, TILES_DEV)

    def forward(vec_b):

        def visit(running, element):
            tile_block, row_ids, col_ids = element
            pieces = vec_b[col_ids].astype(jnp.float32)
            products = jnp.einsum('tij,tj->ti', tile_block.astype(jnp.float32), pieces, precision=lax.Precision.HIGHEST)
            return (running.at[row_ids].add(products), None)
        summed, _ = lax.scan(visit, jnp.zeros((RT, TB), jnp.float32), (flat_tiles, glob_rows, glob_cols))
        return summed

    def backward(vec_b):

        def visit(running, element):
            tile_block, row_ids, col_ids = element
            pieces = vec_b[row_ids].astype(jnp.float32)
            products = jnp.einsum('tij,ti->tj', tile_block.astype(jnp.float32), pieces, precision=lax.Precision.HIGHEST)
            return (running.at[col_ids].add(products), None)
        summed, _ = lax.scan(visit, jnp.zeros((CT, TB), jnp.float32), (flat_tiles, glob_rows, glob_cols))
        return summed
    margin = forward(weights)
    prob = jax.nn.sigmoid(margin)
    curv_weight = prob * (1.0 - prob)
    lam_feat = field_lambda[field_map]
    solution = jnp.zeros((CT, TB), jnp.float32)
    residual = val_grad
    direction = val_grad
    norm_now = jnp.sum(residual * residual)
    for step in range(ITERS):
        dir_b = direction.astype(jnp.bfloat16)
        rows_sum = forward(dir_b)
        scaled_b = (curv_weight * rows_sum).astype(jnp.bfloat16)
        image = backward(scaled_b) + lam_feat * direction
        step_size = norm_now / jnp.sum(direction * image)
        solution = solution + step_size * direction
        residual = residual - step_size * image
        next_norm = jnp.sum(residual * residual)
        direction = residual + next_norm / norm_now * direction
        norm_now = next_norm
    terms = (solution * weights.astype(jnp.float32)).reshape(-1)
    totals = jax.ops.segment_sum(terms, field_map.reshape(-1), num_segments=FIELDS)
    hypergrad = -field_lambda * totals / jnp.sqrt(jnp.float32(NFEAT // FIELDS))
    return (solution, hypergrad)
```

```python
import functools
import math

import jax
import jax.numpy as jnp
from jax import lax
from jax.experimental import pallas as pl
from jax.experimental.pallas import tpu as pltpu
from jax.sharding import PartitionSpec as P

RT_DEV = 2048
ITERS = 3
CAP_ROW = 96
CAP_COL = 64
CHUNKS = 6
GROUP = 16
MESH = pl.DeviceIdType.MESH
F32 = jnp.float32
BF16 = jnp.bfloat16
NN = (((1,), (0,)), ((), ()))
NT = (((1,), (1,)), ((), ()))


def iota(shape, axis):
    return lax.broadcasted_iota(jnp.int32, shape, axis)


def dot(a, b, dims=NN):
    return lax.dot_general(a, b, dims, preferred_element_type=F32)


def fold(x):
    return jnp.sum(x.reshape(-1, 8, x.shape[-1]), axis=0)


def one_hot(cond):
    return jnp.where(cond, 1.0, 0.0).astype(BF16)


def send_all(axis, src, dst, send_sem, recv_sem):
    n = dst.shape[0]
    me = lax.axis_index(axis)

    def one(k, carry):
        peer = lax.rem(me + k, n)
        pltpu.make_async_remote_copy(
            src_ref=src.at[peer], dst_ref=dst.at[me], send_sem=send_sem, recv_sem=recv_sem,
            device_id={axis: peer}, device_id_type=MESH,
        ).start()
        return carry

    lax.fori_loop(1, n, one, 0, unroll=True)
    dst[me] = src[me]


def share_all(axis, value, dst, send_sem, recv_sem):
    n = dst.shape[0]
    me = lax.axis_index(axis)
    dst[me] = value

    def one(k, carry):
        peer = lax.rem(me + k, n)
        pltpu.make_async_remote_copy(
            src_ref=dst.at[me], dst_ref=dst.at[me], send_sem=send_sem, recv_sem=recv_sem,
            device_id={axis: peer}, device_id_type=MESH,
        ).start()
        return carry

    lax.fori_loop(1, n, one, 0, unroll=True)


def drain(axis, dst, send_sem, recv_sem, sent):
    n = dst.shape[0]
    me = lax.axis_index(axis)
    blocks = dst.at[pl.ds(0, n - 1)]
    copy = pltpu.make_async_remote_copy(
        src_ref=blocks, dst_ref=blocks, send_sem=send_sem, recv_sem=recv_sem,
        device_id={axis: lax.rem(me + 1, n)}, device_id_type=MESH,
    )
    if sent:
        copy.wait_send()
    else:
        copy.wait_recv()


def slots(ids, shift, cap, n, s_ref, st_ref):
    nt = ids.shape[1]
    sq0, sq1 = iota((nt, nt), 0), iota((nt, nt), 1)
    eye = sq0 == sq1
    owner_l = (ids >> shift).astype(F32)
    local_l = (ids & ((1 << shift) - 1)).astype(F32)
    owner_s = jnp.sum(jnp.where(eye, owner_l, 0.0), axis=1, keepdims=True)
    local_s = jnp.sum(jnp.where(eye, local_l, 0.0), axis=1, keepdims=True)
    same = owner_s == owner_l
    rank_s = jnp.sum(jnp.where(same & (sq1 < sq0), 1.0, 0.0), axis=1, keepdims=True)
    rank_l = jnp.sum(jnp.where(same & (sq0 < sq1), 1.0, 0.0), axis=0, keepdims=True)
    slot_s = jnp.where(rank_s < cap, owner_s * cap + rank_s, -1.0).astype(jnp.int32)
    slot_l = jnp.where(rank_l < cap, owner_l * cap + rank_l, -1.0).astype(jnp.int32)
    s_ref[...] = one_hot(iota((n * cap, nt), 0) == slot_l)
    st_ref[...] = one_hot(iota((nt, n * cap), 1) == slot_s)
    over = jnp.sum(jnp.where(rank_s < cap, 0.0, 1.0))
    listed = jnp.broadcast_to(local_s + 1.0, (nt, 128)).astype(BF16)
    return over, listed


def tile_groups(count):
    return count // GROUP


def forward_group(tile_ref, base, lhs):
    copies = lhs.shape[0] // GROUP
    row = iota((GROUP, 128), 0)
    accs = [jnp.zeros((GROUP, 128), F32)] * copies
    for k in range(0, GROUP, 2):
        pair = tile_ref[pl.ds(base + k, 2)].reshape(256, 128)
        res = dot(lhs, pair, NT)
        for c in range(copies):
            part = res[c * GROUP:(c + 1) * GROUP]
            accs[c] = jnp.where(row == k, part[:, :128], accs[c])
            accs[c] = jnp.where(row == k + 1, part[:, 128:], accs[c])
    return accs


def forward(tile_ref, piece_ref, out_ref):
    def group(g, carry):
        base = pl.multiple_of(g * GROUP, GROUP)
        (acc,) = forward_group(tile_ref, base, piece_ref[pl.ds(base, GROUP), :])
        out_ref[pl.ds(base, GROUP), :] = acc.astype(out_ref.dtype)
        return carry

    lax.fori_loop(0, tile_groups(tile_ref.shape[0]), group, 0, unroll=8)


def backward(tile_ref, piece_ref, out_ref):
    row = iota((GROUP, 128), 0)
    even = lax.rem(row, 2) == 0

    def group(g, carry):
        base = pl.multiple_of(g * GROUP, GROUP)
        piece = piece_ref[pl.ds(base, GROUP), :]
        zero = jnp.zeros_like(piece)
        lhs = jnp.concatenate([jnp.where(even, piece, zero), jnp.where(even, zero, piece)], axis=1)
        acc = jnp.zeros((GROUP, 128), F32)
        for k in range(0, GROUP, 2):
            pair = tile_ref[pl.ds(base + k, 2)].reshape(256, 128)
            acc = jnp.where((row == k) | (row == k + 1), dot(lhs, pair), acc)
        out_ref[pl.ds(base, GROUP), :] = acc.astype(out_ref.dtype)
        return carry

    lax.fori_loop(0, tile_groups(tile_ref.shape[0]), group, 0, unroll=8)


def split(x):
    high = x.astype(BF16)
    return jnp.concatenate([high, (x - high.astype(F32)).astype(BF16)], axis=1)


def halves(x):
    return x[:, :128] + x[:, 128:]


def kernel(
    dims, row_ids, col_ids, col_smem, lam_smem, tiles_hbm, w_hbm, g_hbm, map_hbm,
    sol_ref, hyp_ref,
    tile, w_b, w_f, g_f, field, piece_w, piece_g, piece_a, prod,
    s_r, st_r, s_c, st_c, m_r, mt_r, m_c, mt_c,
    list_r, list_c, rlist_r, rlist_c,
    part_0, rpart_0, part_r, rpart_r, part_c, rpart_c, gath_r, rgath_r, gath_c, rgath_c,
    red_a, red_a2, red_s, red_s2, red_e, red_e2,
    lam_own, fsum, fields,
    tile_sem, load_sem, send_sem, recv_sem,
):
    nf, ne, nt, own, scale = dims
    e_at = lax.axis_index("ex")

    first = pl.multiple_of(e_at * own, own)
    loads = [
        pltpu.make_async_copy(g_hbm, g_f, load_sem.at[0]),
        pltpu.make_async_copy(w_hbm, w_b, load_sem.at[1]),
        pltpu.make_async_copy(map_hbm.at[pl.ds(first, own)], field, load_sem.at[2]),
    ]
    per = nt // CHUNKS
    for c in range(CHUNKS):
        loads.append(
            pltpu.make_async_copy(
                tiles_hbm.at[pl.ds(c * per, per)], tile.at[pl.ds(c * per, per)], tile_sem.at[c]
            )
        )
    for copy in loads:
        copy.start()
    barrier = pltpu.get_barrier_semaphore()
    for axis, n in (("feat", nf), ("ex", ne)):
        me = lax.axis_index(axis)

        def greet(k, carry, axis=axis, n=n, me=me):
            pl.semaphore_signal(
                barrier, inc=1, device_id={axis: lax.rem(me + k, n)}, device_id_type=MESH
            )
            return carry

        lax.fori_loop(1, n, greet, 0, unroll=True)

    sems = {}

    def sem(name):
        at = sems.setdefault(name, len(sems))
        return send_sem.at[at], recv_sem.at[at]

    pending = []

    def post(axis, src, dst, name):
        send_all(axis, src, dst, *sem(name))
        pending.append((axis, dst, name))

    def share(axis, value, dst, name):
        share_all(axis, value, dst, *sem(name))
        pending.append((axis, dst, name))

    def arrive(axis, dst, name):
        drain(axis, dst, *sem(name), False)

    over_r, local_r = slots(row_ids[...], 8, CAP_ROW, nf, s_r, st_r)
    over_c, local_c = slots(col_ids[...], 8, CAP_COL, ne, s_c, st_c)
    list_r[...] = dot(s_r[...], local_r).astype(BF16).reshape(list_r.shape)
    list_c[...] = dot(s_c[...], local_c).astype(BF16).reshape(list_c.shape)
    pl.semaphore_wait(barrier, nf + ne - 2)
    post("feat", list_r, rlist_r, "list_r")
    post("ex", list_c, rlist_c, "list_c")

    loads[0].wait()
    loads[1].wait()
    w_f[...] = w_b[...].astype(F32)

    def fetch(t, carry):
        at = col_smem[t]
        piece_w[pl.ds(t, 1), :] = w_f[pl.ds(at, 1), :]
        piece_g[pl.ds(t, 1), :] = g_f[pl.ds(at, 1), :]
        return carry

    lax.fori_loop(0, nt, fetch, 0, unroll=16)

    def first_chunk(c):
        def group(g, carry):
            base = pl.multiple_of(c * per + g * GROUP, GROUP)
            rows = pl.ds(base, GROUP)
            lhs = jnp.concatenate(
                [piece_w[rows, :].astype(BF16), piece_g[rows, :].astype(BF16)], axis=0
            )
            piece_w[rows, :], piece_g[rows, :] = forward_group(tile, base, lhs)
            return carry

        lax.fori_loop(0, tile_groups(per), group, 0, unroll=True)

    for c in range(CHUNKS):
        loads[3 + c].wait()
        first_chunk(c)

    def pack(s_ref, x, out):
        out[...] = halves(dot(s_ref[...], split(x))).reshape(out.shape)

    def unpack(m_ref, x):
        return halves(dot(m_ref[...], split(x.reshape(-1, 128))))

    sent_w = halves(dot(s_r[...], split(piece_w[...]))).reshape(nf, CAP_ROW, 128)
    sent_g = halves(dot(s_r[...], split(piece_g[...]))).reshape(nf, CAP_ROW, 128)
    part_0[:, 0] = sent_w
    part_0[:, 1] = sent_g
    post("feat", part_0, rpart_0, "part_0")

    def owner_maps(axis, listed, name, mt_ref, m_ref):
        arrive(axis, listed, name)
        got = listed[...].reshape(-1, 128).astype(F32)
        lane = iota(got.shape, 1).astype(F32)
        for h in range(own // 128):
            half = one_hot(got == lane + (1.0 + 128 * h))
            mt_ref[:, 128 * h:128 * (h + 1)] = half
            m_ref[128 * h:128 * (h + 1), :] = half.T

    owner_maps("feat", rlist_r, "list_r", mt_r, m_r)
    owner_maps("ex", rlist_c, "list_c", mt_c, m_c)
    loads[2].wait()

    def penalties(i, carry):
        rows = pl.ds(pl.multiple_of(i * 32, 32), 32)
        ids = field[rows, :]
        acc = jnp.zeros(ids.shape, F32)
        for k in range(64):
            acc = jnp.where(ids == k, lam_smem[k], acc)
        lam_own[rows, :] = acc
        return carry

    lax.fori_loop(0, own // 32, penalties, 0)
    lam = lam_own[...]
    mine = pl.ds(first, own)
    weights = w_f[mine, :]
    grad = g_f[mine, :]
    fsum[...] = jnp.zeros_like(fsum)

    def field_sums(x, at):
        fields[...] = x * w_f[mine, :]

        def one(k, carry):
            fsum[pl.ds(k, 1), :] = jnp.sum(
                fold(jnp.where(field[...] == k, fields[...], 0.0)), axis=0, keepdims=True
            )
            return carry

        lax.fori_loop(0, 64, one, 0, unroll=4)
        red_e_rows.append(jnp.sum(fsum[...].T, axis=0, keepdims=True))

    red_e_rows = []
    norm = fold(grad * grad)
    field_sums(grad, 0)

    arrive("feat", rpart_0, "part_0")
    margin = unpack(m_r, rpart_0[:, 0])
    prob = jax.nn.sigmoid(margin)
    curv = prob * (1.0 - prob)
    rows_sum = unpack(m_r, rpart_0[:, 1])
    residual = grad
    direction = grad
    sol = jnp.zeros_like(grad)
    beta = None
    reduced = None

    def total(x):
        return jnp.sum(jnp.sum(x, axis=0, keepdims=True), axis=1, keepdims=True)

    over = jnp.broadcast_to(over_r + over_c, (8, 128))
    for step in range(ITERS):
        tag = str(step)
        if step:
            arrive("feat", red_s2.at[2 * step - 2], "nn_f" + str(step - 1))
            next_norm = total(jnp.sum(red_s2[2 * step - 2], axis=0))
            beta = next_norm / norm_all
            norm_all = next_norm
            direction = residual + beta * direction
            arrive("feat", rpart_r.at[step - 1], "part_r" + tag)
            rows_sum = unpack(m_r, rpart_r[step - 1]) + beta * rows_sum
        scaled_b = (curv * rows_sum).astype(BF16)
        bend = fold(rows_sum * scaled_b.astype(F32)) + fold(lam * direction * direction)
        if step + 1 == ITERS:
            break
        gath_r[step] = dot(mt_r[...], scaled_b).astype(BF16).reshape(nf, CAP_ROW, 128)
        post("feat", gath_r.at[step], rgath_r.at[step], "gath_r" + tag)
        if step == 0:
            share("ex", jnp.concatenate([bend, norm, over], axis=0), red_a, "curv_e" + tag)
        else:
            share("ex", bend, red_s.at[2 * step - 1], "curv_e" + tag)

        arrive("feat", rgath_r.at[step], "gath_r" + tag)
        piece_a[...] = dot(st_r[...], rgath_r[step].reshape(-1, 128)).astype(BF16)
        if step == 0:
            arrive("ex", red_a, "curv_e" + tag)
            share("feat", jnp.sum(red_a[...], axis=0), red_a2, "curv_f" + tag)
        else:
            arrive("ex", red_s.at[2 * step - 1], "curv_e" + tag)
            share("feat", jnp.sum(red_s[2 * step - 1], axis=0), red_s2.at[2 * step - 1], "curv_f" + tag)
        backward(tile, piece_a, prod)
        pack(s_c, prod[...], part_c.at[step])
        post("ex", part_c.at[step], rpart_c.at[step], "part_c" + tag)

        if step == 0:
            arrive("feat", red_a2, "curv_f" + tag)
            both = jnp.sum(red_a2[...], axis=0)
            norm_all = total(both[8:16])
            over_all = both[16:24]
            size = norm_all / total(both[:8])
        else:
            arrive("feat", red_s2.at[2 * step - 1], "curv_f" + tag)
            size = norm_all / total(jnp.sum(red_s2[2 * step - 1], axis=0))
        sol = sol + size * direction
        arrive("ex", rpart_c.at[step], "part_c" + tag)
        image = unpack(m_c, rpart_c[step]) + lam * direction
        residual = residual - size * image
        gath_c[step] = dot(mt_c[...], residual.astype(BF16)).astype(BF16).reshape(ne, CAP_COL, 128)
        post("ex", gath_c.at[step], rgath_c.at[step], "gath_c" + tag)
        share("ex", fold(residual * residual), red_s.at[2 * step], "nn_e" + tag)
        field_sums(residual, step + 1)
        arrive("ex", rgath_c.at[step], "gath_c" + tag)
        piece_a[...] = dot(st_c[...], rgath_c[step].reshape(-1, 128)).astype(BF16)
        arrive("ex", red_s.at[2 * step], "nn_e" + tag)
        share("feat", jnp.sum(red_s[2 * step], axis=0), red_s2.at[2 * step], "nn_f" + tag)
        forward(tile, piece_a, prod)
        pack(s_r, prod[...], part_r.at[step])
        post("feat", part_r.at[step], rpart_r.at[step], "part_r" + str(step + 1))
        if step == 0:
            betas = []
            sizes = []
        sizes.append(size)
        if beta is not None:
            betas.append(beta)
    betas.append(beta)

    pad = jnp.zeros((16 - 8 - ITERS, 128), F32)
    share("ex", jnp.concatenate([bend] + red_e_rows + [pad], axis=0), red_e, "end_e")
    arrive("ex", red_e, "end_e")
    share("feat", jnp.sum(red_e[...], axis=0), red_e2, "end_f")
    arrive("feat", red_e2, "end_f")
    last = jnp.sum(red_e2[...], axis=0)
    size = norm_all / total(last[:8])
    sizes.append(size)
    sol_ref[...] = sol + size * direction
    by_dir = last[8:9]
    per_field = sizes[0] * by_dir
    for k in range(1, ITERS):
        by_dir = last[8 + k:9 + k] + betas[k - 1] * by_dir
        per_field = per_field + sizes[k] * by_dir
    lane = iota((1, 128), 1)
    lam_lane = jnp.zeros((1, 128), F32)
    for k in range(64):
        lam_lane = jnp.where(lane == k, lam_smem[k], lam_lane)
    hyper = -lam_lane * per_field * scale
    hyp_ref[...] = jnp.where(iota((8, 128), 0) == 0, jnp.broadcast_to(hyper, (8, 128)), over_all)
    for axis, dst, name in pending:
        drain(axis, dst, *sem(name), True)


def fast(mesh_sizes, tiles, row_index, col_index, weights, val_grad, field_map, field_lambda):
    nf, ne = mesh_sizes
    nt, width = tiles.shape[2], tiles.shape[3]
    segment = weights.shape[0]
    own = segment // ne
    scale = 1.0 / math.sqrt(segment * width * nf // field_lambda.shape[0])
    sr, sc = nf * CAP_ROW, ne * CAP_COL
    vmem, anyspace, smem = (
        pl.BlockSpec(memory_space=pltpu.VMEM),
        pl.BlockSpec(memory_space=pl.ANY),
        pl.BlockSpec(memory_space=pltpu.SMEM),
    )
    steps = ITERS - 1
    scratch = [
        pltpu.VMEM((nt, width, width), BF16),
        pltpu.VMEM((segment, width), BF16),
        pltpu.VMEM((segment, width), F32),
        pltpu.VMEM((segment, width), F32),
        pltpu.VMEM((own, width), jnp.int32),
        pltpu.VMEM((nt, width), F32),
        pltpu.VMEM((nt, width), F32),
        pltpu.VMEM((nt, width), BF16),
        pltpu.VMEM((nt, width), F32),
        pltpu.VMEM((sr, nt), BF16),
        pltpu.VMEM((nt, sr), BF16),
        pltpu.VMEM((sc, nt), BF16),
        pltpu.VMEM((nt, sc), BF16),
        pltpu.VMEM((own, sr), BF16),
        pltpu.VMEM((sr, own), BF16),
        pltpu.VMEM((own, sc), BF16),
        pltpu.VMEM((sc, own), BF16),
    ]
    scratch += [pltpu.VMEM((nf, CAP_ROW, width), BF16), pltpu.VMEM((ne, CAP_COL, width), BF16)] * 2
    scratch += [pltpu.VMEM((nf, 2, CAP_ROW, width), F32)] * 2
    scratch += [pltpu.VMEM((steps, nf, CAP_ROW, width), F32)] * 2
    scratch += [pltpu.VMEM((steps, ne, CAP_COL, width), F32)] * 2
    scratch += [pltpu.VMEM((steps, nf, CAP_ROW, width), BF16)] * 2
    scratch += [pltpu.VMEM((steps, ne, CAP_COL, width), BF16)] * 2
    for rows in (24, None, 16):
        lead = (4,) if rows is None else ()
        scratch += [pltpu.VMEM(lead + (n, rows or 8, width), F32) for n in (ne, nf)]
    scratch += [
        pltpu.VMEM((own, width), F32),
        pltpu.VMEM((width, width), F32),
        pltpu.VMEM((own, width), F32),
        pltpu.SemaphoreType.DMA((CHUNKS,)),
        pltpu.SemaphoreType.DMA((3,)),
        pltpu.SemaphoreType.DMA((24,)),
        pltpu.SemaphoreType.DMA((24,)),
    ]
    cols = col_index.reshape(nt)
    return pl.pallas_call(
        functools.partial(kernel, (nf, ne, nt, own, scale)),
        out_shape=(
            jax.ShapeDtypeStruct((own, width), F32),
            jax.ShapeDtypeStruct((8, width), F32),
        ),
        in_specs=[vmem, vmem, smem, smem, anyspace, anyspace, anyspace, anyspace],
        out_specs=(vmem, vmem),
        scratch_shapes=scratch,
        compiler_params=pltpu.CompilerParams(
            collective_id=0, has_side_effects=True, vmem_limit_bytes=52 << 20
        ),
    )(
        row_index.reshape(1, nt), cols.reshape(1, nt), cols, field_lambda,
        tiles.reshape(nt, width, width), weights, val_grad, field_map,
    )


def general(tiles, row_index, col_index, weights, val_grad, field_map, field_lambda):
    tile_count = tiles.shape[2]
    tile_width = tiles.shape[3]
    tile_stack = tiles.reshape(tile_count, tile_width, tile_width)
    row_ids = row_index.reshape(tile_count)
    col_ids = col_index.reshape(tile_count)
    segment = weights.shape[0]
    share_len = segment // lax.axis_size("ex")
    offset = lax.axis_index("ex") * share_len
    field_count = field_lambda.shape[0]
    labels = jnp.arange(field_count, dtype=jnp.int32)
    norm_scale = 1.0 / math.sqrt(segment * tile_width * lax.axis_size("feat") // field_count)

    def own_part(vector):
        return lax.dynamic_slice_in_dim(vector, offset, share_len, 0)

    def forward(vec_b):
        pieces = jnp.take(vec_b, col_ids, axis=0)
        products = jnp.einsum("tij,tj->ti", tile_stack, pieces, preferred_element_type=jnp.float32)
        partial_rows = jnp.zeros((RT_DEV, tile_width), jnp.float32).at[row_ids].add(products)
        return lax.psum(partial_rows, "feat")

    def lookup(field_block):
        matches = field_block[..., None] == labels
        return jnp.sum(jnp.where(matches, field_lambda, 0.0), axis=-1)

    margin = forward(weights)
    prob = jax.nn.sigmoid(margin)
    curv_weight = prob * (1.0 - prob)
    count = field_map.shape[0]
    block_rows = math.gcd(count, 256)
    lam_part = lax.map(lookup, field_map.reshape(-1, block_rows, tile_width)).reshape(
        count, tile_width
    )
    residual = val_grad

    def local(vector):
        return own_part(vector)

    direction = residual
    solution = jnp.zeros_like(residual)
    dir_b = val_grad.astype(jnp.bfloat16)
    mine = local(residual)
    norm_now = lax.psum(jnp.sum(mine * mine), ("ex", "feat"))
    for step in range(ITERS):
        rows_sum = forward(dir_b)
        scaled_part = (curv_weight * rows_sum).astype(jnp.bfloat16)
        backward_pieces = jnp.take(scaled_part, row_ids, axis=0)
        backward_products = jnp.einsum(
            "tij,ti->tj", tile_stack, backward_pieces, preferred_element_type=jnp.float32
        )
        partial_feat = (
            jnp.zeros((segment, tile_width), jnp.float32).at[col_ids].add(backward_products)
        )
        image = lax.psum(partial_feat, "ex") + lam_part * direction
        own_dir = local(direction)
        own_image = local(image)
        curv_sum = lax.psum(jnp.sum(own_dir * own_image), ("ex", "feat"))
        step_size = norm_now / curv_sum
        solution = solution + step_size * direction
        residual = residual - step_size * image
        if step + 1 < ITERS:
            own_res = local(residual)
            next_norm = lax.psum(jnp.sum(own_res * own_res), ("ex", "feat"))
        if step + 1 < ITERS:
            direction = residual + next_norm / norm_now * direction
            norm_now = next_norm
            dir_b = direction.astype(jnp.bfloat16)
    own_solution = local(solution)
    own_terms = own_solution * own_part(weights).astype(jnp.float32)
    own_fields = own_part(field_map)
    share_block = math.gcd(share_len, 256)

    def field_sums(element):
        term_block, field_block = element
        matches = field_block[..., None] == labels
        return jnp.sum(jnp.where(matches, term_block[..., None], 0.0), axis=(0, 1))

    per_block = lax.map(
        field_sums,
        (
            own_terms.reshape(-1, share_block, tile_width),
            own_fields.reshape(-1, share_block, tile_width),
        ),
    )
    totals = lax.psum(jnp.sum(per_block, axis=0), ("ex", "feat"))
    hypergrad = -field_lambda * totals * norm_scale
    return (own_solution, hypergrad)


def on_device(mesh_sizes, *args):
    own_solution, packed = fast(mesh_sizes, *args)
    fields = args[-1].shape[0]
    return lax.cond(
        packed[1, 0] > 0.5,
        lambda: general(*args),
        lambda: (own_solution, packed[0, :fields]),
    )


def solution(mesh):
    return jax.shard_map(
        functools.partial(on_device, (mesh.shape["feat"], mesh.shape["ex"])),
        mesh=mesh,
        in_specs=(
            P("ex", "feat", None, None, None),
            P("ex", "feat", None),
            P("ex", "feat", None),
            P("feat", None),
            P("feat", None),
            P("feat", None),
            P(),
        ),
        out_specs=(P(("feat", "ex"), None), P()),
        check_vma=False,
    )
```

```python
import functools
import math

import jax
import jax.numpy as jnp
from jax import lax
from jax.experimental import pallas as pl
from jax.experimental.pallas import tpu as pltpu
from jax.sharding import PartitionSpec as P

RT_DEV = 2048
ITERS = 3
CAP_ROW = 96
CAP_COL = 64
CHUNKS = 6
GROUP = 16
MESH = pl.DeviceIdType.MESH
F32 = jnp.float32
LOG2E = 1.4426950408889634
BF16 = jnp.bfloat16
NN = (((1,), (0,)), ((), ()))
NT = (((1,), (1,)), ((), ()))


def iota(shape, axis):
    return lax.broadcasted_iota(jnp.int32, shape, axis)


def dot(a, b, dims=NN):
    return lax.dot_general(a, b, dims, preferred_element_type=F32)


def fold(x):
    return jnp.sum(x.reshape(-1, 8, x.shape[-1]), axis=0)


def one_hot(cond):
    return jnp.where(cond, 1.0, 0.0).astype(BF16)


def send_all(axis, src, dst, send_sem, recv_sem):
    n = dst.shape[0]
    me = lax.axis_index(axis)

    def one(k, carry):
        peer = lax.rem(me + k, n)
        pltpu.make_async_remote_copy(
            src_ref=src.at[peer], dst_ref=dst.at[me], send_sem=send_sem, recv_sem=recv_sem,
            device_id={axis: peer}, device_id_type=MESH,
        ).start()
        return carry

    lax.fori_loop(1, n, one, 0, unroll=True)
    dst[me] = src[me]


def share_all(axis, value, dst, send_sem, recv_sem):
    n = dst.shape[0]
    me = lax.axis_index(axis)
    dst[me] = value

    def one(k, carry):
        peer = lax.rem(me + k, n)
        pltpu.make_async_remote_copy(
            src_ref=dst.at[me], dst_ref=dst.at[me], send_sem=send_sem, recv_sem=recv_sem,
            device_id={axis: peer}, device_id_type=MESH,
        ).start()
        return carry

    lax.fori_loop(1, n, one, 0, unroll=True)


def drain(axis, dst, send_sem, recv_sem, sent):
    n = dst.shape[0]
    me = lax.axis_index(axis)
    blocks = dst.at[pl.ds(0, n - 1)]
    copy = pltpu.make_async_remote_copy(
        src_ref=blocks, dst_ref=blocks, send_sem=send_sem, recv_sem=recv_sem,
        device_id={axis: lax.rem(me + 1, n)}, device_id_type=MESH,
    )
    if sent:
        copy.wait_send()
    else:
        copy.wait_recv()


def slots(ids, shift, cap, n, s_ref, st_ref):
    nt = ids.shape[1]
    sq0, sq1 = iota((nt, nt), 0), iota((nt, nt), 1)
    eye = sq0 == sq1
    owner_l = (ids >> shift).astype(F32)
    local_l = (ids & ((1 << shift) - 1)).astype(F32)
    owner_s = jnp.sum(jnp.where(eye, owner_l, 0.0), axis=1, keepdims=True)
    local_s = jnp.sum(jnp.where(eye, local_l, 0.0), axis=1, keepdims=True)
    same = owner_s == owner_l
    rank_s = jnp.sum(jnp.where(same & (sq1 < sq0), 1.0, 0.0), axis=1, keepdims=True)
    rank_l = jnp.sum(jnp.where(same & (sq0 < sq1), 1.0, 0.0), axis=0, keepdims=True)
    slot_s = jnp.where(rank_s < cap - 1, owner_s * cap + rank_s, -1.0).astype(jnp.int32)
    slot_l = jnp.where(rank_l < cap - 1, owner_l * cap + rank_l, -1.0).astype(jnp.int32)
    s_ref[...] = one_hot(iota((n * cap, nt), 0) == slot_l)
    st_ref[...] = one_hot(iota((nt, n * cap), 1) == slot_s)
    over = jnp.sum(jnp.where(rank_s < cap - 1, 0.0, 1.0))
    listed = jnp.broadcast_to(local_s + 1.0, (nt, 128)).astype(BF16)
    return over, listed


def tile_groups(count):
    return count // GROUP


def forward_group(tile_ref, base, lhs):
    copies = lhs.shape[0] // GROUP
    row = iota((GROUP, 128), 0)
    accs = [jnp.zeros((GROUP, 128), F32)] * copies
    for k in range(0, GROUP, 2):
        pair = tile_ref[pl.ds(base + k, 2)].reshape(256, 128)
        res = dot(lhs, pair, NT)
        for c in range(copies):
            part = res[c * GROUP:(c + 1) * GROUP]
            accs[c] = jnp.where(row == k, part[:, :128], accs[c])
            accs[c] = jnp.where(row == k + 1, part[:, 128:], accs[c])
    return accs


def forward(tile_ref, piece_ref, out_ref):
    def group(g, carry):
        base = pl.multiple_of(g * GROUP, GROUP)
        (acc,) = forward_group(tile_ref, base, piece_ref[pl.ds(base, GROUP), :])
        out_ref[pl.ds(base, GROUP), :] = acc.astype(out_ref.dtype)
        return carry

    lax.fori_loop(0, tile_groups(tile_ref.shape[0]), group, 0, unroll=8)


def backward(tile_ref, piece_ref, out_ref):
    row = iota((GROUP, 128), 0)
    even = lax.rem(row, 2) == 0

    def group(g, carry):
        base = pl.multiple_of(g * GROUP, GROUP)
        piece = piece_ref[pl.ds(base, GROUP), :]
        zero = jnp.zeros_like(piece)
        lhs = jnp.concatenate([jnp.where(even, piece, zero), jnp.where(even, zero, piece)], axis=1)
        acc = jnp.zeros((GROUP, 128), F32)
        for k in range(0, GROUP, 2):
            pair = tile_ref[pl.ds(base + k, 2)].reshape(256, 128)
            acc = jnp.where((row == k) | (row == k + 1), dot(lhs, pair), acc)
        out_ref[pl.ds(base, GROUP), :] = acc.astype(out_ref.dtype)
        return carry

    lax.fori_loop(0, tile_groups(tile_ref.shape[0]), group, 0, unroll=8)


def split(x):
    high = x.astype(BF16)
    return jnp.concatenate([high, (x - high.astype(F32)).astype(BF16)], axis=1)


def halves(x):
    return x[:, :128] + x[:, 128:]


def kernel(
    dims, row_ids, col_ids, col_smem, lam_smem, tiles_hbm, w_hbm, g_hbm, map_hbm,
    sol_ref, hyp_ref,
    tile, w_b, w_f, g_f, field, piece_w, piece_g, piece_a, prod,
    s_r, st_r, s_c, st_c, m_r, mt_r, m_c, mt_c,
    list_r, list_c, rlist_r, rlist_c,
    part_0, rpart_0, part_r, rpart_r, part_c, rpart_c, gath_r, rgath_r, gath_c, rgath_c,
    red_a, red_a2, red_s, red_s2, red_e, red_e2,
    lam_own, fsum, fields,
    tile_sem, load_sem, send_sem, recv_sem,
):
    nf, ne, nt, own, scale = dims
    e_at = lax.axis_index("ex")

    first = pl.multiple_of(e_at * own, own)
    loads = [
        pltpu.make_async_copy(g_hbm, g_f, load_sem.at[0]),
        pltpu.make_async_copy(w_hbm, w_b, load_sem.at[1]),
        pltpu.make_async_copy(map_hbm.at[pl.ds(first, own)], field, load_sem.at[2]),
    ]
    per = nt // CHUNKS
    for c in range(CHUNKS):
        loads.append(
            pltpu.make_async_copy(
                tiles_hbm.at[pl.ds(c * per, per)], tile.at[pl.ds(c * per, per)], tile_sem.at[c]
            )
        )
    for copy in loads:
        copy.start()
    barrier = pltpu.get_barrier_semaphore()
    for axis, n in (("feat", nf), ("ex", ne)):
        me = lax.axis_index(axis)

        def greet(k, carry, axis=axis, n=n, me=me):
            pl.semaphore_signal(
                barrier, inc=1, device_id={axis: lax.rem(me + k, n)}, device_id_type=MESH
            )
            return carry

        lax.fori_loop(1, n, greet, 0, unroll=True)

    sems = {}

    def sem(name):
        at = sems.setdefault(name, len(sems))
        return send_sem.at[at], recv_sem.at[at]

    pending = []

    def post(axis, src, dst, name):
        send_all(axis, src, dst, *sem(name))
        pending.append((axis, dst, name))

    def share(axis, value, dst, name):
        share_all(axis, value, dst, *sem(name))
        pending.append((axis, dst, name))

    def arrive(axis, dst, name):
        drain(axis, dst, *sem(name), False)

    over_r, local_r = slots(row_ids[...], 8, CAP_ROW, nf, s_r, st_r)
    over_c, local_c = slots(col_ids[...], 8, CAP_COL, ne, s_c, st_c)
    list_r[...] = dot(s_r[...], local_r).astype(BF16).reshape(list_r.shape)
    list_c[...] = dot(s_c[...], local_c).astype(BF16).reshape(list_c.shape)
    pl.semaphore_wait(barrier, nf + ne - 2)
    post("feat", list_r, rlist_r, "list_r")
    post("ex", list_c, rlist_c, "list_c")

    loads[0].wait()
    loads[1].wait()
    w_f[...] = w_b[...].astype(F32)

    def fetch(t, carry):
        at = col_smem[t]
        piece_w[pl.ds(t, 1), :] = w_f[pl.ds(at, 1), :]
        piece_g[pl.ds(t, 1), :] = g_f[pl.ds(at, 1), :]
        return carry

    lax.fori_loop(0, nt, fetch, 0, unroll=16)

    def first_chunk(c):
        def group(g, carry):
            base = pl.multiple_of(c * per + g * GROUP, GROUP)
            rows = pl.ds(base, GROUP)
            lhs = jnp.concatenate(
                [piece_w[rows, :].astype(BF16), piece_g[rows, :].astype(BF16)], axis=0
            )
            piece_w[rows, :], piece_g[rows, :] = forward_group(tile, base, lhs)
            return carry

        lax.fori_loop(0, tile_groups(per), group, 0, unroll=True)

    for c in range(CHUNKS):
        loads[3 + c].wait()
        first_chunk(c)

    def pack(s_ref, x, out):
        count, cap, _ = out.shape
        largest = jnp.max(jnp.max(jnp.abs(x), axis=0, keepdims=True), axis=1, keepdims=True)
        exponent = jnp.ceil(jnp.log(jnp.maximum(largest, 1e-30)) * LOG2E)
        exponent = jnp.minimum(jnp.maximum(exponent, -96.0), 120.0)
        fixed = jnp.clip(x * jnp.exp2(15.0 - exponent), -32767.0, 32767.0)
        slotted = halves(dot(s_ref[...], split(jnp.round(fixed)))).reshape(count, cap, 128)
        filled = jnp.where(
            iota((count, cap, 128), 1) == cap - 1, exponent.reshape(1, 1, 1), slotted
        )
        out[...] = filled.astype(jnp.int32).astype(jnp.int16)

    def unpack(m_ref, got):
        x = got[...].astype(jnp.int32).astype(F32)
        cap = x.shape[1]
        x = x * jnp.exp2(x[:, cap - 1:, :] - 15.0)
        return halves(dot(m_ref[...], split(x.reshape(-1, 128))))

    pack(s_r, piece_w[...], part_0.at[0])
    pack(s_r, piece_g[...], part_0.at[1])
    post("feat", part_0.at[0], rpart_0.at[0], "part_w")
    post("feat", part_0.at[1], rpart_0.at[1], "part_g")

    def owner_maps(axis, listed, name, mt_ref, m_ref):
        arrive(axis, listed, name)
        got = listed[...].reshape(-1, 128).astype(F32)
        lane = iota(got.shape, 1).astype(F32)
        for h in range(own // 128):
            half = one_hot(got == lane + (1.0 + 128 * h))
            mt_ref[:, 128 * h:128 * (h + 1)] = half
            m_ref[128 * h:128 * (h + 1), :] = half.T

    owner_maps("feat", rlist_r, "list_r", mt_r, m_r)
    owner_maps("ex", rlist_c, "list_c", mt_c, m_c)
    loads[2].wait()

    def penalties(i, carry):
        rows = pl.ds(pl.multiple_of(i * 32, 32), 32)
        ids = field[rows, :]
        acc = jnp.zeros(ids.shape, F32)
        for k in range(64):
            acc = jnp.where(ids == k, lam_smem[k], acc)
        lam_own[rows, :] = acc
        return carry

    lax.fori_loop(0, own // 32, penalties, 0)
    lam = lam_own[...]
    mine = pl.ds(first, own)
    weights = w_f[mine, :]
    grad = g_f[mine, :]
    fsum[...] = jnp.zeros_like(fsum)

    def field_sums(x, at):
        fields[...] = x * w_f[mine, :]

        def one(k, carry):
            fsum[pl.ds(k, 1), :] = jnp.sum(
                fold(jnp.where(field[...] == k, fields[...], 0.0)), axis=0, keepdims=True
            )
            return carry

        lax.fori_loop(0, 64, one, 0, unroll=4)
        red_e_rows.append(jnp.sum(fsum[...].T, axis=0, keepdims=True))

    red_e_rows = []
    norm = fold(grad * grad)
    field_sums(grad, 0)

    arrive("feat", rpart_0.at[0], "part_w")
    margin = unpack(m_r, rpart_0.at[0])
    prob = jax.nn.sigmoid(margin)
    curv = prob * (1.0 - prob)
    arrive("feat", rpart_0.at[1], "part_g")
    rows_sum = unpack(m_r, rpart_0.at[1])
    residual = grad
    direction = grad
    sol = jnp.zeros_like(grad)
    beta = None
    reduced = None

    def total(x):
        return jnp.sum(jnp.sum(x, axis=0, keepdims=True), axis=1, keepdims=True)

    over = jnp.broadcast_to(over_r + over_c, (8, 128))
    for step in range(ITERS):
        tag = str(step)
        if step:
            arrive("feat", red_s2.at[2 * step - 2], "nn_f" + str(step - 1))
            next_norm = total(jnp.sum(red_s2[2 * step - 2], axis=0))
            beta = next_norm / norm_all
            norm_all = next_norm
            direction = residual + beta * direction
            arrive("feat", rpart_r.at[step - 1], "part_r" + tag)
            rows_sum = unpack(m_r, rpart_r.at[step - 1]) + beta * rows_sum
        scaled_b = (curv * rows_sum).astype(BF16)
        bend = fold(rows_sum * scaled_b.astype(F32)) + fold(lam * direction * direction)
        if step + 1 == ITERS:
            break
        gath_r[step] = dot(mt_r[...], scaled_b).astype(BF16).reshape(nf, CAP_ROW, 128)
        post("feat", gath_r.at[step], rgath_r.at[step], "gath_r" + tag)
        if step == 0:
            share("ex", jnp.concatenate([bend, norm, over], axis=0), red_a, "curv_e" + tag)
        else:
            share("ex", bend, red_s.at[2 * step - 1], "curv_e" + tag)

        arrive("feat", rgath_r.at[step], "gath_r" + tag)
        piece_a[...] = dot(st_r[...], rgath_r[step].reshape(-1, 128)).astype(BF16)
        if step == 0:
            arrive("ex", red_a, "curv_e" + tag)
            share("feat", jnp.sum(red_a[...], axis=0), red_a2, "curv_f" + tag)
        else:
            arrive("ex", red_s.at[2 * step - 1], "curv_e" + tag)
            share("feat", jnp.sum(red_s[2 * step - 1], axis=0), red_s2.at[2 * step - 1], "curv_f" + tag)
        backward(tile, piece_a, prod)
        pack(s_c, prod[...], part_c.at[step])
        post("ex", part_c.at[step], rpart_c.at[step], "part_c" + tag)

        if step == 0:
            arrive("feat", red_a2, "curv_f" + tag)
            both = jnp.sum(red_a2[...], axis=0)
            norm_all = total(both[8:16])
            over_all = both[16:24]
            size = norm_all / total(both[:8])
        else:
            arrive("feat", red_s2.at[2 * step - 1], "curv_f" + tag)
            size = norm_all / total(jnp.sum(red_s2[2 * step - 1], axis=0))
        sol = sol + size * direction
        arrive("ex", rpart_c.at[step], "part_c" + tag)
        image = unpack(m_c, rpart_c.at[step]) + lam * direction
        residual = residual - size * image
        gath_c[step] = dot(mt_c[...], residual.astype(BF16)).astype(BF16).reshape(ne, CAP_COL, 128)
        post("ex", gath_c.at[step], rgath_c.at[step], "gath_c" + tag)
        share("ex", fold(residual * residual), red_s.at[2 * step], "nn_e" + tag)
        field_sums(residual, step + 1)
        arrive("ex", rgath_c.at[step], "gath_c" + tag)
        piece_a[...] = dot(st_c[...], rgath_c[step].reshape(-1, 128)).astype(BF16)
        arrive("ex", red_s.at[2 * step], "nn_e" + tag)
        share("feat", jnp.sum(red_s[2 * step], axis=0), red_s2.at[2 * step], "nn_f" + tag)
        forward(tile, piece_a, prod)
        pack(s_r, prod[...], part_r.at[step])
        post("feat", part_r.at[step], rpart_r.at[step], "part_r" + str(step + 1))
        if step == 0:
            betas = []
            sizes = []
        sizes.append(size)
        if beta is not None:
            betas.append(beta)
    betas.append(beta)

    pad = jnp.zeros((16 - 8 - ITERS, 128), F32)
    share("ex", jnp.concatenate([bend] + red_e_rows + [pad], axis=0), red_e, "end_e")
    arrive("ex", red_e, "end_e")
    share("feat", jnp.sum(red_e[...], axis=0), red_e2, "end_f")
    arrive("feat", red_e2, "end_f")
    last = jnp.sum(red_e2[...], axis=0)
    size = norm_all / total(last[:8])
    sizes.append(size)
    sol_ref[...] = sol + size * direction
    by_dir = last[8:9]
    per_field = sizes[0] * by_dir
    for k in range(1, ITERS):
        by_dir = last[8 + k:9 + k] + betas[k - 1] * by_dir
        per_field = per_field + sizes[k] * by_dir
    lane = iota((1, 128), 1)
    lam_lane = jnp.zeros((1, 128), F32)
    for k in range(64):
        lam_lane = jnp.where(lane == k, lam_smem[k], lam_lane)
    hyper = -lam_lane * per_field * scale
    hyp_ref[...] = jnp.where(iota((8, 128), 0) == 0, jnp.broadcast_to(hyper, (8, 128)), over_all)
    for axis, dst, name in pending:
        drain(axis, dst, *sem(name), True)


def fast(mesh_sizes, tiles, row_index, col_index, weights, val_grad, field_map, field_lambda):
    nf, ne = mesh_sizes
    nt, width = tiles.shape[2], tiles.shape[3]
    segment = weights.shape[0]
    own = segment // ne
    scale = 1.0 / math.sqrt(segment * width * nf // field_lambda.shape[0])
    sr, sc = nf * CAP_ROW, ne * CAP_COL
    vmem, anyspace, smem = (
        pl.BlockSpec(memory_space=pltpu.VMEM),
        pl.BlockSpec(memory_space=pl.ANY),
        pl.BlockSpec(memory_space=pltpu.SMEM),
    )
    steps = ITERS - 1
    scratch = [
        pltpu.VMEM((nt, width, width), BF16),
        pltpu.VMEM((segment, width), BF16),
        pltpu.VMEM((segment, width), F32),
        pltpu.VMEM((segment, width), F32),
        pltpu.VMEM((own, width), jnp.int32),
        pltpu.VMEM((nt, width), F32),
        pltpu.VMEM((nt, width), F32),
        pltpu.VMEM((nt, width), BF16),
        pltpu.VMEM((nt, width), F32),
        pltpu.VMEM((sr, nt), BF16),
        pltpu.VMEM((nt, sr), BF16),
        pltpu.VMEM((sc, nt), BF16),
        pltpu.VMEM((nt, sc), BF16),
        pltpu.VMEM((own, sr), BF16),
        pltpu.VMEM((sr, own), BF16),
        pltpu.VMEM((own, sc), BF16),
        pltpu.VMEM((sc, own), BF16),
    ]
    scratch += [pltpu.VMEM((nf, CAP_ROW, width), BF16), pltpu.VMEM((ne, CAP_COL, width), BF16)] * 2
    scratch += [pltpu.VMEM((2, nf, CAP_ROW, width), jnp.int16)] * 2
    scratch += [pltpu.VMEM((steps, nf, CAP_ROW, width), jnp.int16)] * 2
    scratch += [pltpu.VMEM((steps, ne, CAP_COL, width), jnp.int16)] * 2
    scratch += [pltpu.VMEM((steps, nf, CAP_ROW, width), BF16)] * 2
    scratch += [pltpu.VMEM((steps, ne, CAP_COL, width), BF16)] * 2
    for rows in (24, None, 16):
        lead = (4,) if rows is None else ()
        scratch += [pltpu.VMEM(lead + (n, rows or 8, width), F32) for n in (ne, nf)]
    scratch += [
        pltpu.VMEM((own, width), F32),
        pltpu.VMEM((width, width), F32),
        pltpu.VMEM((own, width), F32),
        pltpu.SemaphoreType.DMA((CHUNKS,)),
        pltpu.SemaphoreType.DMA((3,)),
        pltpu.SemaphoreType.DMA((24,)),
        pltpu.SemaphoreType.DMA((24,)),
    ]
    cols = col_index.reshape(nt)
    return pl.pallas_call(
        functools.partial(kernel, (nf, ne, nt, own, scale)),
        out_shape=(
            jax.ShapeDtypeStruct((own, width), F32),
            jax.ShapeDtypeStruct((8, width), F32),
        ),
        in_specs=[vmem, vmem, smem, smem, anyspace, anyspace, anyspace, anyspace],
        out_specs=(vmem, vmem),
        scratch_shapes=scratch,
        compiler_params=pltpu.CompilerParams(
            collective_id=0, has_side_effects=True, vmem_limit_bytes=52 << 20
        ),
    )(
        row_index.reshape(1, nt), cols.reshape(1, nt), cols, field_lambda,
        tiles.reshape(nt, width, width), weights, val_grad, field_map,
    )


def ring_sum(x, axes):
    for axis in axes:
        n = lax.axis_size(axis)
        me = lax.axis_index(axis)
        around = [(i, (i + 1) % n) for i in range(n)]
        terms = lax.dynamic_update_index_in_dim(jnp.zeros((n,) + x.shape, x.dtype), x, me, 0)

        def hop(k, carry, axis=axis, n=n, me=me, around=around):
            held, terms = carry
            held = lax.ppermute(held, axis, around)
            return held, lax.dynamic_update_index_in_dim(terms, held, lax.rem(me + n - k, n), 0)

        x = jnp.sum(lax.fori_loop(1, n, hop, (x, terms))[1], axis=0)
    return x


def general(tiles, row_index, col_index, weights, val_grad, field_map, field_lambda):
    tile_count = tiles.shape[2]
    tile_width = tiles.shape[3]
    tile_stack = tiles.reshape(tile_count, tile_width, tile_width)
    row_ids = row_index.reshape(tile_count)
    col_ids = col_index.reshape(tile_count)
    segment = weights.shape[0]
    share_len = segment // lax.axis_size("ex")
    offset = lax.axis_index("ex") * share_len
    field_count = field_lambda.shape[0]
    labels = jnp.arange(field_count, dtype=jnp.int32)
    norm_scale = 1.0 / math.sqrt(segment * tile_width * lax.axis_size("feat") // field_count)

    def own_part(vector):
        return lax.dynamic_slice_in_dim(vector, offset, share_len, 0)

    def forward(vec_b):
        pieces = jnp.take(vec_b, col_ids, axis=0)
        products = jnp.einsum("tij,tj->ti", tile_stack, pieces, preferred_element_type=jnp.float32)
        partial_rows = jnp.zeros((RT_DEV, tile_width), jnp.float32).at[row_ids].add(products)
        return ring_sum(partial_rows, ("feat",))

    def lookup(field_block):
        matches = field_block[..., None] == labels
        return jnp.sum(jnp.where(matches, field_lambda, 0.0), axis=-1)

    margin = forward(weights)
    prob = jax.nn.sigmoid(margin)
    curv_weight = prob * (1.0 - prob)
    count = field_map.shape[0]
    block_rows = math.gcd(count, 256)
    lam_part = lax.map(lookup, field_map.reshape(-1, block_rows, tile_width)).reshape(
        count, tile_width
    )
    residual = val_grad

    def local(vector):
        return own_part(vector)

    direction = residual
    solution = jnp.zeros_like(residual)
    dir_b = val_grad.astype(jnp.bfloat16)
    mine = local(residual)
    norm_now = ring_sum(jnp.sum(mine * mine), ("ex", "feat"))
    for step in range(ITERS):
        rows_sum = forward(dir_b)
        scaled_part = (curv_weight * rows_sum).astype(jnp.bfloat16)
        backward_pieces = jnp.take(scaled_part, row_ids, axis=0)
        backward_products = jnp.einsum(
            "tij,ti->tj", tile_stack, backward_pieces, preferred_element_type=jnp.float32
        )
        partial_feat = (
            jnp.zeros((segment, tile_width), jnp.float32).at[col_ids].add(backward_products)
        )
        image = ring_sum(partial_feat, ("ex",)) + lam_part * direction
        own_dir = local(direction)
        own_image = local(image)
        curv_sum = ring_sum(jnp.sum(own_dir * own_image), ("ex", "feat"))
        step_size = norm_now / curv_sum
        solution = solution + step_size * direction
        residual = residual - step_size * image
        if step + 1 < ITERS:
            own_res = local(residual)
            next_norm = ring_sum(jnp.sum(own_res * own_res), ("ex", "feat"))
        if step + 1 < ITERS:
            direction = residual + next_norm / norm_now * direction
            norm_now = next_norm
            dir_b = direction.astype(jnp.bfloat16)
    own_solution = local(solution)
    own_terms = own_solution * own_part(weights).astype(jnp.float32)
    own_fields = own_part(field_map)
    share_block = math.gcd(share_len, 256)

    def field_sums(element):
        term_block, field_block = element
        matches = field_block[..., None] == labels
        return jnp.sum(jnp.where(matches, term_block[..., None], 0.0), axis=(0, 1))

    per_block = lax.map(
        field_sums,
        (
            own_terms.reshape(-1, share_block, tile_width),
            own_fields.reshape(-1, share_block, tile_width),
        ),
    )
    totals = ring_sum(jnp.sum(per_block, axis=0), ("ex", "feat"))
    hypergrad = -field_lambda * totals * norm_scale
    return (own_solution, hypergrad)


def on_device(mesh_sizes, *args):
    own_solution, packed = fast(mesh_sizes, *args)
    fields = args[-1].shape[0]
    return lax.cond(
        packed[1, 0] > 0.5,
        lambda: general(*args),
        lambda: (own_solution, packed[0, :fields]),
    )


def solution(mesh):
    return jax.shard_map(
        functools.partial(on_device, (mesh.shape["feat"], mesh.shape["ex"])),
        mesh=mesh,
        in_specs=(
            P("ex", "feat", None, None, None),
            P("ex", "feat", None),
            P("ex", "feat", None),
            P("feat", None),
            P("feat", None),
            P("feat", None),
            P(),
        ),
        out_specs=(P(("feat", "ex"), None), P()),
        check_vma=False,
    )
```
